32 devices in a mesh: band: 4 (over y, core), grid: 8 (over z, x).
Axes of the slice: x: 2, y: 2, z: 4, core: 2. Of those that a mesh axis runs over, the one named last changes fastest.
Arguments:
- orbitals: float32 [64, 16, 4096], P('band', 'grid'), may hold values from -6 to 6
- potential: float32 [16, 4096], P('grid'), may hold values from 0 to 2
Outputs:
- rotated: bfloat16 [64, 16, 4096], P('band', 'grid')
The draws below stay inside these ranges and needn't reach their ends.
All inputs are finite; a program needn't handle non-finite values. Where the reference program divides by a largest or mean magnitude, that divisor is 1e-20 or more.
Results may differ from the reference program's by a relative error of at most 0.001.
The reference program's roundings to bfloat16 on the way (of `filtered` and `root`) count: a program that leaves them out, or rounds other values in their place, can miss the bound.
Values may be sent and summed in bfloat16 or wider, within the bound.
A program may use at most 64 MiB of HBM per device.

```python
import jax
import jax.numpy as jnp
from jax import lax

NX = 64
PLANE = 4096
NZ = 16
CELLS = 65536
ORB_DEV = 16
ORBS = 64
DEGREE = 2
NS_ITERS = 2


def raised(values, key, source, target, blocks, factor):
    def block_of(axis_at):
        return (jnp.arange(values.shape[axis_at]) // (values.shape[axis_at] // blocks)).reshape((-1,) + (1,) * (values.ndim - 1 - axis_at))

    near = jax.random.permutation(key, blocks)[block_of(target)]
    second = (block_of(target) + blocks // 2) % blocks
    return jnp.where((block_of(source) == near) | (block_of(source) == second), factor * values, values)


def steps_of(key, extent, cuts, low, largest):
    level = 1.0
    for axis_at, parts in cuts:
        heights = jax.random.uniform(jax.random.fold_in(jax.random.fold_in(key, 6), axis_at), (parts,), jnp.float32, low / len(cuts), largest / len(cuts))
        level = level * jnp.repeat(jnp.exp(heights), extent[axis_at] // parts).reshape((-1,) + (1,) * (len(extent) - 1 - axis_at))
    return level


def noise_with(key, dims, scale, most, split, heavy, kind=jnp.bfloat16):
    drawn = scale * jax.random.normal(key, dims, jnp.float32)
    if split:
        drawn = drawn * steps_of(key, dims, split, -0.22, 0.18)
    return jnp.clip(raised(drawn, jax.random.fold_in(key, 3), *heavy), -most, most).astype(kind)


def setup_inputs(seed: int = 0) -> dict:
    key_list = jax.random.split(jax.random.key(seed), 3)
    orbitals = noise_with(key_list[0], (ORBS, NZ, PLANE), 1.0, 6.0, ((0, 4), (1, 8)), (1, 0, 8, 2.0), jnp.float32)
    potential = jnp.clip(2.0 * jax.random.uniform(key_list[1], (NZ, PLANE), jnp.float32) ** steps_of(key_list[1], (NZ, PLANE), ((0, 8),), -0.2, 0.2), 0.0, 2.0)
    return dict(orbitals=orbitals, potential=potential)


def hamiltonian(field, potential):
    cube = field.reshape(field.shape[0], NZ, NX, NX)
    beside = jnp.roll(cube, 1, 1) + jnp.roll(cube, -1, 1)
    beside = beside + jnp.roll(cube, 1, 2) + jnp.roll(cube, -1, 2)
    beside = beside + jnp.roll(cube, 1, 3) + jnp.roll(cube, -1, 3)
    beside = beside.reshape(field.shape)
    return 0.5 * (6.0 * field - beside) + potential[None] * field

def filter_block(block, potential):
    previous = block
    current = block
    for degree_step in range(DEGREE):
        applied = hamiltonian(current, potential)
        if degree_step == 0:
            following = (applied - 5.0 * current) / 3.0
        else:
            following = 2.0 * (applied - 5.0 * current) / 3.0 - previous
        previous = current
        current = following
    return current.astype(jnp.bfloat16)

def reference(orbitals, potential):
    blocks = orbitals.reshape(ORBS // ORB_DEV, ORB_DEV, NZ, PLANE)
    filtered = lax.map(lambda block: filter_block(block, potential), blocks)
    flat = filtered.reshape(ORBS, NZ * PLANE)
    gram = lax.dot_general(flat, flat, (((1,), (1,)), ((), ())), preferred_element_type=jnp.float32) / CELLS
    scale = jnp.max(lax.optimization_barrier(jnp.sum(jnp.abs(gram), axis=1)))
    identity_mat = jnp.eye(ORBS, dtype=jnp.float32)
    upper = gram / scale
    lower = identity_mat
    for sweep in range(NS_ITERS):
        factor = 1.5 * identity_mat - 0.5 * jnp.dot(lower, upper, precision=lax.Precision.HIGHEST)
        upper = jnp.dot(upper, factor, precision=lax.Precision.HIGHEST)
        lower = jnp.dot(factor, lower, precision=lax.Precision.HIGHEST)
    root = (lower / jnp.sqrt(scale)).astype(jnp.bfloat16)
    rotated = lax.dot_general(root, flat, (((0,), (0,)), ((), ())), preferred_element_type=jnp.float32)
    return rotated.astype(jnp.bfloat16).reshape(ORBS, NZ, PLANE)
```

```python
import functools

import jax
import jax.numpy as jnp
from jax import lax
from jax.experimental import pallas as pl
from jax.experimental.pallas import tpu as pltpu
from jax.sharding import PartitionSpec as P

NX = 64
DEGREE = 2
NS_ITERS = 2


def with_halo(block, sides, width):
    for axis, dim in sides:
        count = lax.axis_size(axis)
        forward = [(i, i + 1) for i in range(count - 1)]
        forward.append((count - 1, 0))
        backward = [(target, source) for source, target in forward]
        low = lax.ppermute(
            lax.slice_in_dim(block, block.shape[dim] - width, None, axis=dim), axis, forward
        )
        high = lax.ppermute(lax.slice_in_dim(block, 0, width, axis=dim), axis, backward)
        block = jnp.concatenate([low, block, high], axis=dim)
    return block


def apply_inner(extended, potential):
    inner = extended[:, 1:-1]
    count = inner.shape[0]
    planes = inner.shape[1]
    square = inner.reshape(count, planes, NX, NX)
    sideways = jnp.roll(square, 1, 2) + jnp.roll(square, -1, 2)
    sideways = sideways + jnp.roll(square, 1, 3) + jnp.roll(square, -1, 3)
    beside = extended[:, 2:] + extended[:, :-2] + sideways.reshape(inner.shape)
    return 0.5 * (6.0 * inner - beside) + potential[None] * inner


def remote(src, dst, send, recv, **where):
    return pltpu.make_async_remote_copy(
        src_ref=src, dst_ref=dst, send_sem=send, recv_sem=recv,
        device_id=where, device_id_type=pl.DeviceIdType.MESH,
    )


def newton_schulz(gram):
    size = gram.shape[0]
    scale = jnp.max(jnp.sum(jnp.abs(gram), axis=1, keepdims=True), axis=0, keepdims=True)
    rows = lax.broadcasted_iota(jnp.int32, (size, size), 0)
    cols = lax.broadcasted_iota(jnp.int32, (size, size), 1)
    identity_mat = (rows == cols).astype(jnp.float32)
    upper = gram / scale
    lower = None
    for sweep in range(NS_ITERS):
        product = upper if lower is None else jnp.dot(
            lower, upper, precision=lax.Precision.HIGHEST, preferred_element_type=jnp.float32)
        factor = 1.5 * identity_mat - 0.5 * product
        if sweep < NS_ITERS - 1:
            upper = jnp.dot(upper, factor, precision=lax.Precision.HIGHEST,
                            preferred_element_type=jnp.float32)
        lower = factor if lower is None else jnp.dot(
            factor, lower, precision=lax.Precision.HIGHEST, preferred_element_type=jnp.float32)
    return lower / jnp.sqrt(scale)


def exchange(n, axis, me, src_of, dst_of, send, recv):
    sends = []
    for step in range(1, n):
        peer = lax.rem(me + step, n)
        copy = remote(src_of(peer), dst_of(me), send.at[step], recv.at[step], **{axis: peer})
        copy.start()
        sends.append(copy)

    def arrived():
        for step in range(1, n):
            source = lax.rem(me + n - step, n)
            remote(src_of(source), dst_of(source), send.at[step], recv.at[step],
                   **{axis: source}).wait_recv()

    def sent():
        for copy in sends:
            copy.wait_send()

    return arrived, sent


def rows_of(index, size):
    return pl.ds(pl.multiple_of(index * size, size), size)


def tail(nb, ng, count, filt_ref, out_ref, pieces, turned, gpart, rs, gr, gfull,
         own_sem, s0, r0, s1, r1, s2, r2, s3, r3, s4, r4):
    orbs = nb * count
    share = pieces.shape[1]
    total_cells = share * nb * ng
    b = lax.axis_index("band")
    g = lax.axis_index("grid")
    own = pltpu.make_async_copy(
        filt_ref.at[:, rows_of(b, share)], pieces.at[rows_of(b, count)], own_sem.at[0])
    own.start()
    arrived, sent = exchange(
        nb, "band", b, lambda p: filt_ref.at[:, rows_of(p, share)],
        lambda p: pieces.at[rows_of(p, count)], s0, r0)
    gpart[...] = jnp.zeros_like(gpart)
    own.wait()
    arrived()
    everything = pieces[...]
    gpart[:, :orbs] = lax.dot_general(
        everything, everything, (((1,), (1,)), ((), ())),
        preferred_element_type=jnp.float32) / total_cells
    arrived1, sent1 = exchange(
        nb, "band", b, lambda p: gpart.at[rows_of(p, count)], lambda p: rs.at[p], s1, r1)
    rs[b] = gpart[rows_of(b, count), :]
    arrived1()
    gr[g] = jnp.sum(rs[...], axis=0)
    arrived2, sent2 = exchange(ng, "grid", g, lambda p: gr.at[g], lambda p: gr.at[p], s2, r2)
    arrived2()
    gfull[rows_of(b, count), :] = jnp.sum(gr[...], axis=0)
    arrived3, sent3 = exchange(
        nb, "band", b, lambda p: gfull.at[rows_of(b, count)],
        lambda p: gfull.at[rows_of(p, count)], s3, r3)
    arrived3()
    root = newton_schulz(gfull[:, :orbs]).astype(jnp.bfloat16)
    turned[...] = lax.dot_general(
        root, pieces[...], (((0,), (0,)), ((), ())),
        preferred_element_type=jnp.float32).astype(jnp.bfloat16)
    back = pltpu.make_async_copy(
        turned.at[rows_of(b, count)], out_ref.at[:, rows_of(b, share)], own_sem.at[1])
    back.start()
    arrived4, sent4 = exchange(
        nb, "band", b, lambda p: turned.at[rows_of(p, count)],
        lambda p: out_ref.at[:, rows_of(p, share)], s4, r4)
    arrived4()
    back.wait()
    for done in (sent, sent1, sent2, sent3, sent4):
        done()


def greet(nb, ng):
    b = lax.axis_index("band")
    g = lax.axis_index("grid")
    barrier = pltpu.get_barrier_semaphore()
    for step in range(1, nb):
        pl.semaphore_signal(barrier, inc=1, device_id={"band": lax.rem(b + step, nb)},
                            device_id_type=pl.DeviceIdType.MESH)
    for step in range(1, ng):
        pl.semaphore_signal(barrier, inc=1, device_id={"grid": lax.rem(g + step, ng)},
                            device_id_type=pl.DeviceIdType.MESH)
    pl.semaphore_wait(barrier, nb + ng - 2)


def kernel(nb, ng, count, filt_ref, out_ref, *rest):
    greet(nb, ng)
    tail(nb, ng, count, filt_ref, out_ref, *rest)


def tail_scratch(nb, ng, count, cells):
    orbs = nb * count
    wide = max(128, orbs)
    share = cells // nb
    return [
        pltpu.VMEM((orbs, share), jnp.bfloat16),
        pltpu.VMEM((orbs, share), jnp.bfloat16),
        pltpu.VMEM((orbs, wide), jnp.float32),
        pltpu.VMEM((nb, count, wide), jnp.float32),
        pltpu.VMEM((ng, count, wide), jnp.float32),
        pltpu.VMEM((orbs, wide), jnp.float32),
        pltpu.SemaphoreType.DMA((2,)),
        pltpu.SemaphoreType.DMA((nb,)), pltpu.SemaphoreType.DMA((nb,)),
        pltpu.SemaphoreType.DMA((nb,)), pltpu.SemaphoreType.DMA((nb,)),
        pltpu.SemaphoreType.DMA((ng,)), pltpu.SemaphoreType.DMA((ng,)),
        pltpu.SemaphoreType.DMA((nb,)), pltpu.SemaphoreType.DMA((nb,)),
        pltpu.SemaphoreType.DMA((nb,)), pltpu.SemaphoreType.DMA((nb,)),
    ]


def local(orbitals, potential):
    previous = orbitals
    current = orbitals
    for degree_step in range(DEGREE):
        extended = with_halo(current, (("grid", 1),), 1)
        applied = apply_inner(extended, potential)
        if degree_step == 0:
            following = (applied - 5.0 * current) / 3.0
        else:
            following = 2.0 * (applied - 5.0 * current) / 3.0 - previous
        previous = current
        current = following
    count, zplanes, width = orbitals.shape
    cells = zplanes * width
    nb = lax.axis_size("band")
    ng = lax.axis_size("grid")
    filtered = current.astype(jnp.bfloat16).reshape(count, cells)
    returned = pl.pallas_call(
        functools.partial(kernel, nb, ng, count),
        out_shape=jax.ShapeDtypeStruct((count, cells), jnp.bfloat16),
        in_specs=[pl.BlockSpec(memory_space=pltpu.VMEM)],
        out_specs=pl.BlockSpec(memory_space=pltpu.VMEM),
        scratch_shapes=tail_scratch(nb, ng, count, cells),
        compiler_params=pltpu.CompilerParams(collective_id=0, has_side_effects=True),
    )(filtered)
    return returned.reshape(count, zplanes, width)


def solution(mesh):
    placed = (P("band", "grid", None), P("grid", None))
    return jax.shard_map(
        local, mesh=mesh, in_specs=placed, out_specs=P("band", "grid", None), check_vma=False
    )
```

```python
import functools

import jax
import jax.numpy as jnp
from jax import lax
from jax.experimental import pallas as pl
from jax.experimental.pallas import tpu as pltpu
from jax.sharding import PartitionSpec as P

NS_ITERS = 2
LANES = 128
HALF = LANES // 2


def remote(src, dst, send, recv, **where):
    return pltpu.make_async_remote_copy(
        src_ref=src, dst_ref=dst, send_sem=send, recv_sem=recv,
        device_id=where, device_id_type=pl.DeviceIdType.MESH,
    )


def newton_schulz(gram):
    size = gram.shape[0]
    scale = jnp.max(jnp.sum(jnp.abs(gram), axis=1, keepdims=True), axis=0, keepdims=True)
    rows = lax.broadcasted_iota(jnp.int32, (size, size), 0)
    cols = lax.broadcasted_iota(jnp.int32, (size, size), 1)
    identity_mat = (rows == cols).astype(jnp.float32)
    upper = gram / scale
    lower = None
    for sweep in range(NS_ITERS):
        product = upper if lower is None else jnp.dot(
            lower, upper, precision=lax.Precision.HIGHEST, preferred_element_type=jnp.float32)
        factor = 1.5 * identity_mat - 0.5 * product
        if sweep < NS_ITERS - 1:
            upper = jnp.dot(upper, factor, precision=lax.Precision.HIGHEST,
                            preferred_element_type=jnp.float32)
        lower = factor if lower is None else jnp.dot(
            factor, lower, precision=lax.Precision.HIGHEST, preferred_element_type=jnp.float32)
    return lower / jnp.sqrt(scale)


def exchange(n, axis, me, src_of, dst_of, send, recv):
    sends = []
    for step in range(1, n):
        peer = lax.rem(me + step, n)
        copy = remote(src_of(peer), dst_of(me), send.at[step], recv.at[step], **{axis: peer})
        copy.start()
        sends.append(copy)

    def arrived():
        for step in range(1, n):
            source = lax.rem(me + n - step, n)
            remote(src_of(source), dst_of(source), send.at[step], recv.at[step],
                   **{axis: source}).wait_recv()

    def sent():
        for copy in sends:
            copy.wait_send()

    return arrived, sent


def rows_of(index, size):
    return pl.ds(pl.multiple_of(index * size, size), size)


def sideways(block, lane, before, after):
    turned = pltpu.roll(block, HALF, 1)
    inner = lane % HALF
    below = pltpu.roll(jnp.where(inner == HALF - 1, turned, block), 1, 1)
    above = pltpu.roll(jnp.where(inner == 0, turned, block), LANES - 1, 1)
    rows = turned + pltpu.roll(jnp.where(lane >= HALF, before, after), HALF, 1)
    return rows + (below + above)


def filter_planes(width, pot, slab, first, filt, firsts, seconds):
    blocks = width // LANES

    def columns(index):
        return pl.ds(pl.multiple_of(index * LANES, LANES), LANES)

    def at(plane):
        return slab.at[plane // 2, plane % 2]

    lane = lax.broadcasted_iota(jnp.int32, (slab.shape[2], LANES), 1)

    def places(index):
        return (columns(index), columns(lax.rem(index + blocks - 1, blocks)),
                columns(lax.rem(index + 1, blocks)))

    def level(plane, here):
        return (pot[plane // 2, pl.ds(plane % 2, 1), here] - 2.0) * (1.0 / 3.0)

    def step1(index, carry):
        here, before, after = places(index)
        for plane in firsts:
            ref = at(plane)
            beside = sideways(ref[:, here], lane, ref[:, before], ref[:, after])
            beside = beside + (at(plane - 1)[:, here] + at(plane + 1)[:, here])
            first[plane, :, here] = level(plane, here) * ref[:, here] - beside * (1.0 / 6.0)
        return carry

    def step2(index, carry):
        here, before, after = places(index)
        for plane in seconds:
            ref = first.at[plane]
            beside = sideways(ref[:, here], lane, ref[:, before], ref[:, after])
            beside = beside + (first[plane - 1, :, here] + first[plane + 1, :, here])
            value = 2.0 * level(plane, here) * ref[:, here] - beside * (1.0 / 3.0)
            filt[plane - 2, :, here] = (value - at(plane)[:, here]).astype(jnp.bfloat16)
        return carry

    if firsts:
        lax.fori_loop(0, blocks, step1, 0, unroll=2)
    if seconds:
        lax.fori_loop(0, blocks, step2, 0, unroll=2)


def kernel(nb, ng, orb_ref, pot_ref, out_ref, slab, pot, first, filt, parts,
           pieces, turned, gpart, rs, gr, gfull, own_sem, hs, hr, ps, pr, fs, fr,
           s1, r1, s2, r2, s3, r3, s4, r4):
    count, width = orb_ref.shape[1:]
    half = count // 2
    orbs = nb * count
    share = pieces.shape[1]
    per_plane = nb // 2
    pairs = ng // 2
    total_cells = share * nb * ng
    b = lax.axis_index("band")
    g = lax.axis_index("grid")
    pair = g // 2
    h = g % 2
    other = 1 - h
    partner = 2 * pair + other
    low = 2 * lax.rem(pair + pairs - 1, pairs)
    high = 2 * lax.rem(pair + 1, pairs)
    target = 2 * lax.rem(pair + pairs - 1 + 2 * h, pairs)
    slot = 3 - 3 * h

    barrier = pltpu.get_barrier_semaphore()
    for step in range(1, ng):
        pl.semaphore_signal(barrier, inc=1, device_id={"grid": lax.rem(g + step, ng)},
                            device_id_type=pl.DeviceIdType.MESH)
    for step in range(1, nb):
        for where in (g, partner):
            pl.semaphore_signal(
                barrier, inc=1, device_id={"band": lax.rem(b + step, nb), "grid": where},
                device_id_type=pl.DeviceIdType.MESH)

    def orbital_rows(index):
        return orb_ref.at[:, rows_of(index, half)]

    own = [pltpu.make_async_copy(orbital_rows(h), slab.at[1 + h], own_sem.at[0]),
           pltpu.make_async_copy(pot_ref, pot.at[1 + h], own_sem.at[1])]
    for copy in own:
        copy.start()
    pl.semaphore_wait(barrier, ng - 1 + 2 * (nb - 1))

    def across(index, where, to_slot, send):
        return [
            remote(orbital_rows(index), slab.at[to_slot], hs.at[send], hr.at[to_slot], grid=where),
            remote(pot_ref, pot.at[to_slot], ps.at[send], pr.at[to_slot], grid=where)]

    moves = (across(h, target + h, slot, 0) + across(other, partner, 1 + h, 1)
             + across(other, target + other, slot, 2))
    for copy in moves:
        copy.start()

    def landed(source, from_slot):
        for copy in across(h, source, from_slot, 0):
            copy.wait_recv()

    for copy in own:
        copy.wait()
    landed(partner, 2 - h)
    filter_planes(width, pot, slab, first, filt, (3, 4), ())
    landed(low + 1, 0)
    filter_planes(width, pot, slab, first, filt, (1, 2), (2, 3))
    landed(high, 3)
    filter_planes(width, pot, slab, first, filt, (5, 6), (4, 5))

    def cells_for(to_h, to_b):
        return filt.at[2 * to_h + to_b // per_plane, :,
                       rows_of(to_b % per_plane, share)]

    mine = pltpu.make_async_copy(cells_for(h, b), parts.at[b, h], own_sem.at[2])
    mine.start()
    spread = []
    for dh in (1, 0):
        for db in range(nb):
            if dh + db:
                to_h = (h + dh) % 2
                to_b = lax.rem(b + db, nb)
                copy = remote(cells_for(to_h, to_b), parts.at[b, h], fs.at[dh * nb + db],
                              fr.at[dh * nb + db], band=to_b, grid=2 * pair + to_h)
                copy.start()
                spread.append(copy)
    gpart[...] = jnp.zeros_like(gpart)
    mine.wait()
    for dh in (0, 1):
        for db in range(nb):
            if dh + db:
                from_h = (h + dh) % 2
                from_b = lax.rem(b + nb - db, nb)
                remote(cells_for(from_h, from_b), parts.at[from_b, from_h], fs.at[dh * nb + db],
                       fr.at[dh * nb + db], band=from_b, grid=2 * pair + from_h).wait_recv()
    for index in range(nb):
        both = jnp.concatenate([parts[index, 0].astype(jnp.float32),
                                parts[index, 1].astype(jnp.float32)], axis=0)
        pieces[index * count:(index + 1) * count, :] = both.astype(jnp.bfloat16)
    everything = pieces[...]
    gpart[:, :orbs] = lax.dot_general(
        everything, everything, (((1,), (1,)), ((), ())),
        preferred_element_type=jnp.float32) / total_cells
    arrived1, sent1 = exchange(
        nb, "band", b, lambda p: gpart.at[rows_of(p, count)], lambda p: rs.at[p], s1, r1)
    rs[b] = gpart[rows_of(b, count), :]
    arrived1()
    gr[g] = jnp.sum(rs[...], axis=0)
    arrived2, sent2 = exchange(ng, "grid", g, lambda p: gr.at[g], lambda p: gr.at[p], s2, r2)
    arrived2()
    gfull[rows_of(b, count), :] = jnp.sum(gr[...], axis=0)
    arrived3, sent3 = exchange(
        nb, "band", b, lambda p: gfull.at[rows_of(b, count)],
        lambda p: gfull.at[rows_of(p, count)], s3, r3)
    arrived3()
    root = newton_schulz(gfull[:, :orbs]).astype(jnp.bfloat16)
    turned[...] = lax.dot_general(
        root, pieces[...], (((0,), (0,)), ((), ())),
        preferred_element_type=jnp.float32).astype(jnp.bfloat16)
    back = pltpu.make_async_copy(
        turned.at[rows_of(b, count)], out_ref.at[:, rows_of(b, share)], own_sem.at[3])
    back.start()
    arrived4, sent4 = exchange(
        nb, "band", b, lambda p: turned.at[rows_of(p, count)],
        lambda p: out_ref.at[:, rows_of(p, share)], s4, r4)
    arrived4()
    back.wait()
    for copy in moves + spread:
        copy.wait_send()
    for done in (sent1, sent2, sent3, sent4):
        done()


def local(orbitals, potential):
    count, zplanes, width = orbitals.shape
    cells = zplanes * width
    nb = lax.axis_size("band")
    ng = lax.axis_size("grid")
    half = count // 2
    orbs = nb * count
    wide = max(LANES, orbs)
    share = cells // nb
    bf16, f32 = jnp.bfloat16, jnp.float32
    dma = pltpu.SemaphoreType.DMA
    returned = pl.pallas_call(
        functools.partial(kernel, nb, ng),
        out_shape=jax.ShapeDtypeStruct((count, cells), bf16),
        in_specs=[pl.BlockSpec(memory_space=pltpu.VMEM)] * 2,
        out_specs=pl.BlockSpec(memory_space=pltpu.VMEM),
        scratch_shapes=[
            pltpu.VMEM((4, zplanes, half, width), f32),
            pltpu.VMEM((4, zplanes, width), f32),
            pltpu.VMEM((8, half, width), f32),
            pltpu.VMEM((4, half, width), bf16),
            pltpu.VMEM((nb, 2, half, share), bf16),
            pltpu.VMEM((orbs, share), bf16),
            pltpu.VMEM((orbs, share), bf16),
            pltpu.VMEM((orbs, wide), f32),
            pltpu.VMEM((nb, count, wide), f32),
            pltpu.VMEM((ng, count, wide), f32),
            pltpu.VMEM((orbs, wide), f32),
            dma((4,)), dma((3,)), dma((4,)), dma((3,)), dma((4,)), dma((2 * nb,)), dma((2 * nb,)),
            dma((nb,)), dma((nb,)), dma((ng,)), dma((ng,)),
            dma((nb,)), dma((nb,)), dma((nb,)), dma((nb,)),
        ],
        compiler_params=pltpu.CompilerParams(collective_id=0, has_side_effects=True),
    )(jnp.swapaxes(orbitals, 0, 1), potential)
    return returned.reshape(count, zplanes, width)


def solution(mesh):
    placed = (P("band", "grid", None), P("grid", None))
    return jax.shard_map(
        local, mesh=mesh, in_specs=placed, out_specs=P("band", "grid", None), check_vma=False
    )
```

```python
import functools

import jax
import jax.numpy as jnp
from jax import lax
from jax.experimental import pallas as pl
from jax.experimental.pallas import tpu as pltpu
from jax.sharding import PartitionSpec as P

NS_ITERS = 2
LANES = 128
HALF = LANES // 2


def remote(src, dst, send, recv, **where):
    return pltpu.make_async_remote_copy(
        src_ref=src, dst_ref=dst, send_sem=send, recv_sem=recv,
        device_id=where, device_id_type=pl.DeviceIdType.MESH,
    )


def newton_schulz(gram):
    size = gram.shape[0]
    scale = jnp.max(jnp.sum(jnp.abs(gram), axis=1, keepdims=True), axis=0, keepdims=True)
    rows = lax.broadcasted_iota(jnp.int32, (size, size), 0)
    cols = lax.broadcasted_iota(jnp.int32, (size, size), 1)
    identity_mat = (rows == cols).astype(jnp.float32)
    upper = gram / scale
    lower = None
    for sweep in range(NS_ITERS):
        product = upper if lower is None else jnp.dot(
            lower, upper, precision=lax.Precision.HIGHEST, preferred_element_type=jnp.float32)
        factor = 1.5 * identity_mat - 0.5 * product
        if sweep < NS_ITERS - 1:
            upper = jnp.dot(upper, factor, precision=lax.Precision.HIGHEST,
                            preferred_element_type=jnp.float32)
        lower = factor if lower is None else jnp.dot(
            factor, lower, precision=lax.Precision.HIGHEST, preferred_element_type=jnp.float32)
    return lower / jnp.sqrt(scale)


def exchange(n, axis, me, src_of, dst_of, send, recv):
    sends = []
    for step in range(1, n):
        peer = lax.rem(me + step, n)
        copy = remote(src_of(peer), dst_of(me), send.at[step], recv.at[step], **{axis: peer})
        copy.start()
        sends.append(copy)

    def arrived():
        for step in range(1, n):
            source = lax.rem(me + n - step, n)
            remote(src_of(source), dst_of(source), send.at[step], recv.at[step],
                   **{axis: source}).wait_recv()

    def sent():
        for copy in sends:
            copy.wait_send()

    return arrived, sent


def rows_of(index, size):
    return pl.ds(pl.multiple_of(index * size, size), size)


def sideways(block, lane, before, after):
    turned = pltpu.roll(block, HALF, 1)
    inner = lane % HALF
    below = pltpu.roll(jnp.where(inner == HALF - 1, turned, block), 1, 1)
    above = pltpu.roll(jnp.where(inner == 0, turned, block), LANES - 1, 1)
    rows = turned + pltpu.roll(jnp.where(lane >= HALF, before, after), HALF, 1)
    return rows + (below + above)


def filter_planes(width, pot, slab, first, filt, firsts, seconds):
    blocks = width // LANES

    def columns(index):
        return pl.ds(pl.multiple_of(index * LANES, LANES), LANES)

    def at(plane):
        return slab.at[plane // 2, plane % 2]

    lane = lax.broadcasted_iota(jnp.int32, (slab.shape[2], LANES), 1)

    def places(index):
        return (columns(index), columns(lax.rem(index + blocks - 1, blocks)),
                columns(lax.rem(index + 1, blocks)))

    def level(plane, here):
        return (pot[plane // 2, pl.ds(plane % 2, 1), here] - 2.0) * (1.0 / 3.0)

    def step1(index, carry):
        here, before, after = places(index)
        for plane in firsts:
            ref = at(plane)
            beside = sideways(ref[:, here], lane, ref[:, before], ref[:, after])
            beside = beside + (at(plane - 1)[:, here] + at(plane + 1)[:, here])
            first[plane, :, here] = level(plane, here) * ref[:, here] - beside * (1.0 / 6.0)
        return carry

    def step2(index, carry):
        here, before, after = places(index)
        for plane in seconds:
            ref = first.at[plane]
            beside = sideways(ref[:, here], lane, ref[:, before], ref[:, after])
            beside = beside + (first[plane - 1, :, here] + first[plane + 1, :, here])
            value = 2.0 * level(plane, here) * ref[:, here] - beside * (1.0 / 3.0)
            filt[plane - 2, :, here] = (value - at(plane)[:, here]).astype(jnp.bfloat16)
        return carry

    if firsts:
        lax.fori_loop(0, blocks, step1, 0, unroll=16)
    if seconds:
        lax.fori_loop(0, blocks, step2, 0, unroll=16)


def kernel(nb, ng, orb_ref, pot_ref, out_ref, raw, slab, pot, first, filt, parts,
           pieces, turned, gpart, rs, gr, gfull, landing, spaced, own_sem, hs, hr, ps, pr, fs, fr,
           s1, r1, s2, r2, s3, r3, s4, r4):
    half, width = slab.shape[2:]
    count = 2 * half
    deep = 2 * width // LANES
    orbs = nb * count
    share = pieces.shape[1]
    per_plane = nb // 2
    pairs = ng // 2
    total_cells = share * nb * ng
    b = lax.axis_index("band")
    g = lax.axis_index("grid")
    pair = g // 2
    h = g % 2
    other = 1 - h
    partner = 2 * pair + other
    low = 2 * lax.rem(pair + pairs - 1, pairs)
    high = 2 * lax.rem(pair + 1, pairs)
    target = 2 * lax.rem(pair + pairs - 1 + 2 * h, pairs)
    slot = 3 - 3 * h

    barrier = pltpu.get_barrier_semaphore()
    for step in range(1, ng):
        pl.semaphore_signal(barrier, inc=1, device_id={"grid": lax.rem(g + step, ng)},
                            device_id_type=pl.DeviceIdType.MESH)
    for step in range(1, nb):
        for where in (g, partner):
            pl.semaphore_signal(
                barrier, inc=1, device_id={"band": lax.rem(b + step, nb), "grid": where},
                device_id_type=pl.DeviceIdType.MESH)

    def orbital_rows(index):
        return orb_ref.at[rows_of(index, half * deep)]

    own = [pltpu.make_async_copy(orbital_rows(h), raw.at[1 + h], own_sem.at[0]),
           pltpu.make_async_copy(pot_ref, pot.at[1 + h], own_sem.at[1])]
    for copy in own:
        copy.start()
    pl.semaphore_wait(barrier, ng - 1 + 2 * (nb - 1))

    def across(index, where, to_slot, send):
        return [
            remote(orbital_rows(index), raw.at[to_slot], hs.at[send], hr.at[to_slot], grid=where),
            remote(pot_ref, pot.at[to_slot], ps.at[send], pr.at[to_slot], grid=where)]

    moves = (across(h, target + h, slot, 0) + across(other, partner, 1 + h, 1)
             + across(other, target + other, slot, 2))
    for copy in moves:
        copy.start()

    def unpack(at_slot):
        def column(index, carry):
            where = pl.ds(pl.multiple_of(index * LANES, LANES), LANES)
            for plane in range(2):
                slab[at_slot, plane, :, where] = raw[
                    at_slot, pl.ds(2 * index + plane, half, stride=deep), :]
            return carry

        lax.fori_loop(0, width // LANES, column, 0, unroll=8)

    def landed(source, from_slot):
        for copy in across(h, source, from_slot, 0):
            copy.wait_recv()

    for copy in own:
        copy.wait()
    unpack(1 + h)
    landed(partner, 2 - h)
    unpack(2 - h)
    filter_planes(width, pot, slab, first, filt, (3, 4), ())
    landed(low + 1, 0)
    unpack(0)
    filter_planes(width, pot, slab, first, filt, (1, 2), (2, 3))
    landed(high, 3)
    unpack(3)
    filter_planes(width, pot, slab, first, filt, (5, 6), (4, 5))

    def cells_for(to_h, to_b):
        return filt.at[2 * to_h + to_b // per_plane, :,
                       rows_of(to_b % per_plane, share)]

    mine = pltpu.make_async_copy(cells_for(h, b), parts.at[b, h], own_sem.at[2])
    mine.start()
    spread = []
    for dh in (1, 0):
        for db in range(nb):
            if dh + db:
                to_h = (h + dh) % 2
                to_b = lax.rem(b + db, nb)
                copy = remote(cells_for(to_h, to_b), parts.at[b, h], fs.at[dh * nb + db],
                              fr.at[dh * nb + db], band=to_b, grid=2 * pair + to_h)
                copy.start()
                spread.append(copy)
    gpart[...] = jnp.zeros_like(gpart)
    mine.wait()
    for dh in (0, 1):
        for db in range(nb):
            if dh + db:
                from_h = (h + dh) % 2
                from_b = lax.rem(b + nb - db, nb)
                remote(cells_for(from_h, from_b), parts.at[from_b, from_h], fs.at[dh * nb + db],
                       fr.at[dh * nb + db], band=from_b, grid=2 * pair + from_h).wait_recv()
    for index in range(nb):
        both = jnp.concatenate([parts[index, 0].astype(jnp.float32),
                                parts[index, 1].astype(jnp.float32)], axis=0)
        pieces[index * count:(index + 1) * count, :] = both.astype(jnp.bfloat16)
    everything = pieces[...]
    gpart[:, :orbs] = lax.dot_general(
        everything, everything, (((1,), (1,)), ((), ())),
        preferred_element_type=jnp.float32) / total_cells
    arrived1, sent1 = exchange(
        nb, "band", b, lambda p: gpart.at[rows_of(p, count)], lambda p: rs.at[p], s1, r1)
    rs[b] = gpart[rows_of(b, count), :]
    arrived1()
    gr[g] = jnp.sum(rs[...], axis=0)
    arrived2, sent2 = exchange(ng, "grid", g, lambda p: gr.at[g], lambda p: gr.at[p], s2, r2)
    arrived2()
    gfull[rows_of(b, count), :] = jnp.sum(gr[...], axis=0)
    arrived3, sent3 = exchange(
        nb, "band", b, lambda p: gfull.at[rows_of(b, count)],
        lambda p: gfull.at[rows_of(p, count)], s3, r3)
    arrived3()
    root = newton_schulz(gfull[:, :orbs]).astype(jnp.bfloat16)
    turned[...] = lax.dot_general(
        root, pieces[...], (((0,), (0,)), ((), ())),
        preferred_element_type=jnp.float32).astype(jnp.bfloat16)
    arrived4, sent4 = exchange(
        nb, "band", b, lambda p: turned.at[rows_of(p, count)], lambda p: landing.at[p], s4, r4)

    def place(owner, block):
        blocks = share // LANES
        base = 2 * blocks * (owner % per_plane) + owner // per_plane
        for index in range(blocks):
            values = block[:, index * LANES:(index + 1) * LANES].astype(jnp.float32)
            for part in range(2):
                spaced[pl.ds(part * half * deep + base + 2 * index, half, stride=deep), :] = (
                    values[part * half:(part + 1) * half])

    place(b, turned[rows_of(b, count), :])
    for step in range(1, nb):
        source = lax.rem(b + nb - step, nb)
        remote(turned.at[rows_of(source, count)], landing.at[source], s4.at[step], r4.at[step],
               band=source).wait_recv()
        place(source, landing[source])
    out_ref[...] = spaced[...].astype(jnp.bfloat16)
    for copy in moves + spread:
        copy.wait_send()
    for done in (sent1, sent2, sent3, sent4):
        done()


def local(orbitals, potential):
    count, zplanes, width = orbitals.shape
    cells = zplanes * width
    nb = lax.axis_size("band")
    ng = lax.axis_size("grid")
    half = count // 2
    orbs = nb * count
    wide = max(LANES, orbs)
    share = cells // nb
    bf16, f32 = jnp.bfloat16, jnp.float32
    dma = pltpu.SemaphoreType.DMA
    returned = pl.pallas_call(
        functools.partial(kernel, nb, ng),
        out_shape=jax.ShapeDtypeStruct((count * cells // LANES, LANES), bf16),
        in_specs=[pl.BlockSpec(memory_space=pl.ANY)] * 2,
        out_specs=pl.BlockSpec(memory_space=pltpu.VMEM),
        scratch_shapes=[
            pltpu.VMEM((4, half * cells // LANES, LANES), f32),
            pltpu.VMEM((4, zplanes, half, width), f32),
            pltpu.VMEM((4, zplanes, width), f32),
            pltpu.VMEM((8, half, width), f32),
            pltpu.VMEM((4, half, width), bf16),
            pltpu.VMEM((nb, 2, half, share), bf16),
            pltpu.VMEM((orbs, share), bf16),
            pltpu.VMEM((orbs, share), bf16),
            pltpu.VMEM((orbs, wide), f32),
            pltpu.VMEM((nb, count, wide), f32),
            pltpu.VMEM((ng, count, wide), f32),
            pltpu.VMEM((orbs, wide), f32),
            pltpu.VMEM((nb, count, share), bf16),
            pltpu.VMEM((count * cells // LANES, LANES), f32),
            dma((4,)), dma((3,)), dma((4,)), dma((3,)), dma((4,)), dma((2 * nb,)), dma((2 * nb,)),
            dma((nb,)), dma((nb,)), dma((ng,)), dma((ng,)),
            dma((nb,)), dma((nb,)), dma((nb,)), dma((nb,)),
        ],
        compiler_params=pltpu.CompilerParams(collective_id=0, has_side_effects=True),
    )(orbitals.reshape(count, zplanes, width // LANES, LANES).swapaxes(1, 2).reshape(-1, LANES),
      potential)
    spread = returned.reshape(count, width // LANES, zplanes, LANES).swapaxes(1, 2)
    return spread.reshape(count, zplanes, width)


def solution(mesh):
    placed = (P("band", "grid", None), P("grid", None))
    return jax.shard_map(
        local, mesh=mesh, in_specs=placed, out_specs=P("band", "grid", None), check_vma=False
    )
```

```python
import functools

import jax
import jax.numpy as jnp
from jax import lax
from jax.experimental import pallas as pl
from jax.experimental.pallas import tpu as pltpu
from jax.sharding import PartitionSpec as P

NS_ITERS = 2
LANES = 128
HALF = LANES // 2


def remote(src, dst, send, recv, **where):
    return pltpu.make_async_remote_copy(
        src_ref=src, dst_ref=dst, send_sem=send, recv_sem=recv,
        device_id=where, device_id_type=pl.DeviceIdType.MESH,
    )


def newton_schulz(gram):
    size = gram.shape[0]
    scale = jnp.max(jnp.sum(jnp.abs(gram), axis=1, keepdims=True), axis=0, keepdims=True)
    rows = lax.broadcasted_iota(jnp.int32, (size, size), 0)
    cols = lax.broadcasted_iota(jnp.int32, (size, size), 1)
    identity_mat = (rows == cols).astype(jnp.float32)
    upper = gram / scale
    lower = None
    for sweep in range(NS_ITERS):
        product = upper if lower is None else jnp.dot(
            lower, upper, precision=lax.Precision.HIGHEST, preferred_element_type=jnp.float32)
        factor = 1.5 * identity_mat - 0.5 * product
        if sweep < NS_ITERS - 1:
            upper = jnp.dot(upper, factor, precision=lax.Precision.HIGHEST,
                            preferred_element_type=jnp.float32)
        lower = factor if lower is None else jnp.dot(
            factor, lower, precision=lax.Precision.HIGHEST, preferred_element_type=jnp.float32)
    return lower / jnp.sqrt(scale)


def exchange(n, axis, me, src_of, dst_of, send, recv):
    sends = []
    for step in range(1, n):
        peer = lax.rem(me + step, n)
        copy = remote(src_of(peer), dst_of(me), send.at[step], recv.at[step], **{axis: peer})
        copy.start()
        sends.append(copy)

    def arrived():
        for step in range(1, n):
            source = lax.rem(me + n - step, n)
            remote(src_of(source), dst_of(source), send.at[step], recv.at[step],
                   **{axis: source}).wait_recv()

    def sent():
        for copy in sends:
            copy.wait_send()

    return arrived, sent


def rows_of(index, size):
    return pl.ds(pl.multiple_of(index * size, size), size)


def sideways(block, lane, before, after):
    turned = pltpu.roll(block, HALF, 1)
    inner = lane % HALF
    below = pltpu.roll(jnp.where(inner == HALF - 1, turned, block), 1, 1)
    above = pltpu.roll(jnp.where(inner == 0, turned, block), LANES - 1, 1)
    rows = turned + pltpu.roll(jnp.where(lane >= HALF, before, after), HALF, 1)
    return rows + (below + above)


def filter_planes(width, pot, slab, first, filt, firsts, seconds):
    blocks = width // LANES

    def columns(index):
        return pl.ds(pl.multiple_of(index * LANES, LANES), LANES)

    def at(plane):
        return slab.at[plane // 2, plane % 2]

    lane = lax.broadcasted_iota(jnp.int32, (slab.shape[2], LANES), 1)

    def places(index):
        return (columns(index), columns(lax.rem(index + blocks - 1, blocks)),
                columns(lax.rem(index + 1, blocks)))

    def level(plane, here):
        return (pot[plane // 2, pl.ds(plane % 2, 1), here] - 2.0) * (1.0 / 3.0)

    def step1(index, carry):
        here, before, after = places(index)
        for plane in firsts:
            ref = at(plane)
            beside = sideways(ref[:, here], lane, ref[:, before], ref[:, after])
            beside = beside + (at(plane - 1)[:, here] + at(plane + 1)[:, here])
            first[plane, :, here] = level(plane, here) * ref[:, here] - beside * (1.0 / 6.0)
        return carry

    def step2(index, carry):
        here, before, after = places(index)
        for plane in seconds:
            ref = first.at[plane]
            beside = sideways(ref[:, here], lane, ref[:, before], ref[:, after])
            beside = beside + (first[plane - 1, :, here] + first[plane + 1, :, here])
            value = 2.0 * level(plane, here) * ref[:, here] - beside * (1.0 / 3.0)
            filt[plane - 2, :, here] = (value - at(plane)[:, here]).astype(jnp.bfloat16)
        return carry

    if firsts:
        lax.fori_loop(0, blocks, step1, 0, unroll=16)
    if seconds:
        lax.fori_loop(0, blocks, step2, 0, unroll=16)


def kernel(nb, ng, orb_ref, pot_ref, out_ref, raw, slab, pot, first, filt, parts,
           pieces, turned, gpart, rs, gr, gfull, landing, spaced, own_sem, hs, hr, ps, pr, fs, fr,
           s1, r1, s2, r2, s3, r3, s4, r4):
    half, width = slab.shape[2:]
    count = 2 * half
    deep = 2 * width // LANES
    orbs = nb * count
    share = pieces.shape[1]
    per_plane = nb // 2
    pairs = ng // 2
    total_cells = share * nb * ng
    b = lax.axis_index("band")
    g = lax.axis_index("grid")
    pair = g // 2
    h = g % 2
    other = 1 - h
    partner = 2 * pair + other
    low = 2 * lax.rem(pair + pairs - 1, pairs)
    high = 2 * lax.rem(pair + 1, pairs)
    target = 2 * lax.rem(pair + pairs - 1 + 2 * h, pairs)
    slot = 3 - 3 * h

    barrier = pltpu.get_barrier_semaphore()
    for step in range(1, ng):
        pl.semaphore_signal(barrier, inc=1, device_id={"grid": lax.rem(g + step, ng)},
                            device_id_type=pl.DeviceIdType.MESH)
    for step in range(1, nb):
        for where in (g, partner):
            pl.semaphore_signal(
                barrier, inc=1, device_id={"band": lax.rem(b + step, nb), "grid": where},
                device_id_type=pl.DeviceIdType.MESH)

    def orbital_rows(index):
        return orb_ref.at[rows_of(index, half * deep)]

    own = [pltpu.make_async_copy(orbital_rows(h), raw.at[1 + h], own_sem.at[0]),
           pltpu.make_async_copy(pot_ref, pot.at[1 + h], own_sem.at[1])]
    for copy in own:
        copy.start()
    pl.semaphore_wait(barrier, ng - 1 + 2 * (nb - 1))

    def across(index, where, to_slot, send):
        return [
            remote(orbital_rows(index), raw.at[to_slot], hs.at[send], hr.at[to_slot], grid=where),
            remote(pot_ref, pot.at[to_slot], ps.at[send], pr.at[to_slot], grid=where)]

    moves = (across(h, target + h, slot, 0) + across(other, partner, 1 + h, 1)
             + across(other, target + other, slot, 2))
    for copy in moves:
        copy.start()

    def unpack(at_slot):
        def column(index, carry):
            where = pl.ds(pl.multiple_of(index * LANES, LANES), LANES)
            for plane in range(2):
                slab[at_slot, plane, :, where] = raw[
                    at_slot, pl.ds(2 * index + plane, half, stride=deep), :]
            return carry

        lax.fori_loop(0, width // LANES, column, 0, unroll=8)

    def landed(source, from_slot):
        for copy in across(h, source, from_slot, 0):
            copy.wait_recv()

    for copy in own:
        copy.wait()
    unpack(1 + h)
    landed(partner, 2 - h)
    unpack(2 - h)
    filter_planes(width, pot, slab, first, filt, (3, 4), ())
    landed(low + 1, 0)
    unpack(0)
    filter_planes(width, pot, slab, first, filt, (1, 2), (2, 3))
    landed(high, 3)
    unpack(3)
    filter_planes(width, pot, slab, first, filt, (5, 6), (4, 5))

    def cells_for(to_h, to_b):
        return filt.at[2 * to_h + to_b // per_plane, :,
                       rows_of(to_b % per_plane, share)]

    mine = pltpu.make_async_copy(cells_for(h, b), parts.at[b, h], own_sem.at[2])
    mine.start()
    spread = []
    for dh in (1, 0):
        for db in range(nb):
            if dh + db:
                to_h = (h + dh) % 2
                to_b = lax.rem(b + db, nb)
                copy = remote(cells_for(to_h, to_b), parts.at[b, h], fs.at[dh * nb + db],
                              fr.at[dh * nb + db], band=to_b, grid=2 * pair + to_h)
                copy.start()
                spread.append(copy)
    mine.wait()
    for dh in (0, 1):
        for db in range(nb):
            if dh + db:
                from_h = (h + dh) % 2
                from_b = lax.rem(b + nb - db, nb)
                remote(cells_for(from_h, from_b), parts.at[from_b, from_h], fs.at[dh * nb + db],
                       fr.at[dh * nb + db], band=from_b, grid=2 * pair + from_h).wait_recv()
    for index in range(nb):
        both = jnp.concatenate([parts[index, 0].astype(jnp.float32),
                                parts[index, 1].astype(jnp.float32)], axis=0)
        pieces[index * count:(index + 1) * count, :] = both.astype(jnp.bfloat16)
    everything = pieces[...]
    gram = lax.dot_general(
        everything, everything, (((1,), (1,)), ((), ())),
        preferred_element_type=jnp.float32) / total_cells
    rows = gpart.shape[1]
    fold = count // rows
    for index in range(nb):
        for part in range(fold):
            start = index * count + part * rows
            gpart[index, :, part * orbs:(part + 1) * orbs] = gram[start:start + rows]
    arrived1, sent1 = exchange(
        nb, "band", b, lambda p: gpart.at[p], lambda p: rs.at[p], s1, r1)
    rs[b] = gpart[b]
    arrived1()
    gr[g] = jnp.sum(rs[...], axis=0)
    arrived2, sent2 = exchange(ng, "grid", g, lambda p: gr.at[g], lambda p: gr.at[p], s2, r2)
    arrived2()
    gfull[b] = jnp.sum(gr[...], axis=0)
    arrived3, sent3 = exchange(
        nb, "band", b, lambda p: gfull.at[b], lambda p: gfull.at[p], s3, r3)
    arrived3()
    gram = jnp.concatenate(
        [gfull[index, :, part * orbs:(part + 1) * orbs]
         for index in range(nb) for part in range(fold)], axis=0)
    root = newton_schulz(gram).astype(jnp.bfloat16)
    turned[...] = lax.dot_general(
        root, pieces[...], (((0,), (0,)), ((), ())),
        preferred_element_type=jnp.float32).astype(jnp.bfloat16)
    arrived4, sent4 = exchange(
        nb, "band", b, lambda p: turned.at[rows_of(p, count)], lambda p: landing.at[p], s4, r4)

    def place(owner, block):
        blocks = share // LANES
        base = 2 * blocks * (owner % per_plane) + owner // per_plane
        for index in range(blocks):
            values = block[:, index * LANES:(index + 1) * LANES].astype(jnp.float32)
            for part in range(2):
                spaced[pl.ds(part * half * deep + base + 2 * index, half, stride=deep), :] = (
                    values[part * half:(part + 1) * half])

    place(b, turned[rows_of(b, count), :])
    for step in range(1, nb):
        source = lax.rem(b + nb - step, nb)
        remote(turned.at[rows_of(source, count)], landing.at[source], s4.at[step], r4.at[step],
               band=source).wait_recv()
        place(source, landing[source])
    out_ref[...] = spaced[...].astype(jnp.bfloat16)
    for copy in moves + spread:
        copy.wait_send()
    for done in (sent1, sent2, sent3, sent4):
        done()


def local(orbitals, potential):
    count, zplanes, width = orbitals.shape
    cells = zplanes * width
    nb = lax.axis_size("band")
    ng = lax.axis_size("grid")
    half = count // 2
    orbs = nb * count
    fold = 2 if 2 * orbs == LANES else 1
    wide = fold * orbs
    packed = count // fold
    share = cells // nb
    bf16, f32 = jnp.bfloat16, jnp.float32
    dma = pltpu.SemaphoreType.DMA
    returned = pl.pallas_call(
        functools.partial(kernel, nb, ng),
        out_shape=jax.ShapeDtypeStruct((count * cells // LANES, LANES), bf16),
        in_specs=[pl.BlockSpec(memory_space=pl.ANY)] * 2,
        out_specs=pl.BlockSpec(memory_space=pltpu.VMEM),
        scratch_shapes=[
            pltpu.VMEM((4, half * cells // LANES, LANES), f32),
            pltpu.VMEM((4, zplanes, half, width), f32),
            pltpu.VMEM((4, zplanes, width), f32),
            pltpu.VMEM((8, half, width), f32),
            pltpu.VMEM((4, half, width), bf16),
            pltpu.VMEM((nb, 2, half, share), bf16),
            pltpu.VMEM((orbs, share), bf16),
            pltpu.VMEM((orbs, share), bf16),
            pltpu.VMEM((nb, packed, wide), f32),
            pltpu.VMEM((nb, packed, wide), f32),
            pltpu.VMEM((ng, packed, wide), f32),
            pltpu.VMEM((nb, packed, wide), f32),
            pltpu.VMEM((nb, count, share), bf16),
            pltpu.VMEM((count * cells // LANES, LANES), f32),
            dma((4,)), dma((3,)), dma((4,)), dma((3,)), dma((4,)), dma((2 * nb,)), dma((2 * nb,)),
            dma((nb,)), dma((nb,)), dma((ng,)), dma((ng,)),
            dma((nb,)), dma((nb,)), dma((nb,)), dma((nb,)),
        ],
        compiler_params=pltpu.CompilerParams(collective_id=0, has_side_effects=True,
                                             vmem_limit_bytes=16 * 2**20),
    )(orbitals.reshape(count, zplanes, width // LANES, LANES).swapaxes(1, 2).reshape(-1, LANES),
      potential)
    spread = returned.reshape(count, width // LANES, zplanes, LANES).swapaxes(1, 2)
    return spread.reshape(count, zplanes, width)


def solution(mesh):
    placed = (P("band", "grid", None), P("grid", None))
    return jax.shard_map(
        local, mesh=mesh, in_specs=placed, out_specs=P("band", "grid", None), check_vma=False
    )
```
